128 devices in a mesh: chan: 8 (over x_hi, z), filt: 16 (over y, x_lo, core).
Axes of the slice: x: 4 (x_hi: 2, x_lo: 2; x = x_hi * 2 + x_lo), y: 4, z: 4, core: 2. Of those that a mesh axis runs over, the one named last changes fastest.
Arguments:
- inputs: bfloat16 [1, 16, 16, 16, 2048], P(None, 'chan', 'filt'), may hold values from -6 to 6
- filters: bfloat16 [3, 3, 3, 2048, 2048], P(None, None, None, 'chan', 'filt'), may hold values from -0.02734375 to 0.02734375
- cotangent: bfloat16 [1, 16, 16, 16, 2048], P(None, 'chan', None, None, 'filt'), may hold values from -6 to 6
Outputs:
- outputs: bfloat16 [1, 16, 16, 16, 2048], P(None, 'chan', None, None, 'filt')
- input_grad: bfloat16 [1, 16, 16, 16, 2048], P(None, None, 'filt', None, 'chan')
- filter_grad: float32 [3, 3, 3, 2048, 2048], P(None, None, None, 'chan', 'filt')
The draws below stay inside these ranges and needn't reach their ends.
All inputs are finite; a program needn't handle non-finite values.
Results may differ from the reference program's by a relative error of at most 0.001.
Values may be sent and summed in bfloat16 or wider, within the bound.
No kernel may reach another device: no remote copies, remote signals or barrier semaphores. Data moves between devices by JAX's collectives and lax.ppermute only.
A program may use at most 128 MiB of HBM per device.

```python
import jax
import jax.numpy as jnp
from jax import lax

C = 2048
F = 2048
S = 16
BATCH = 1


def steps_of(key, dims, split, smallest, high):
    level, own = 1.0, jax.random.fold_in(key, 6)
    for axis_at, blocks in split:
        draws = jnp.exp(jax.random.uniform(jax.random.fold_in(own, axis_at), (blocks,), jnp.float32, smallest / len(split), high / len(split)))
        level = level * jnp.repeat(draws, dims[axis_at] // blocks).reshape([-1 if axis == axis_at else 1 for axis in range(len(dims))])
    return level


def scatter_about(own_key, shape, spread, reach, cuts=(), held_as=jnp.bfloat16):
    loudness = steps_of(own_key, shape, cuts, -0.22, 0.18) if cuts else 1.0
    array = jax.random.normal(own_key, shape, jnp.float32) * spread * loudness
    return jnp.minimum(jnp.maximum(array, -reach), reach).astype(held_as)


def setup_inputs(seed: int = 0) -> dict:
    keys = jax.random.split(jax.random.key(seed), 4)
    return {
        "inputs": scatter_about(keys[0], (BATCH, S, S, S, C), 1.0, 6.0, ((1, 8), (2, 16))),
        "filters": scatter_about(keys[1], (3, 3, 3, C, F), (27 * C) ** -0.5, 0.02734375, ((3, 8), (4, 16))),
        "cotangent": scatter_about(keys[2], (BATCH, S, S, S, F), 1.0, 6.0, ((1, 8), (4, 16))),
    }


def reference(inputs, filters, cotangent):
    values = inputs.astype(jnp.float32)
    grads = cotangent.astype(jnp.float32)
    weights = filters.astype(jnp.float32)
    out_total = jnp.zeros(cotangent.shape, jnp.float32)
    grad_total = jnp.zeros(inputs.shape, jnp.float32)
    weight_taps = []
    for tap_index in range(27):
        shift_z = tap_index // 9 - 1
        shift_y = (tap_index // 3) % 3 - 1
        shift_x = tap_index % 3 - 1
        kernel = weights[tap_index // 9, (tap_index // 3) % 3, tap_index % 3]
        shifted = jnp.roll(values, (-shift_z, -shift_y, -shift_x), axis=(1, 2, 3))
        out_total = out_total + jnp.einsum("nzyxc,cf->nzyxf", shifted, kernel, precision=lax.Precision.HIGHEST)
        weight_taps.append(jnp.einsum("nzyxc,nzyxf->cf", shifted, grads, precision=lax.Precision.HIGHEST))
        back = jnp.roll(grads, (shift_z, shift_y, shift_x), axis=(1, 2, 3))
        grad_total = grad_total + jnp.einsum("nzyxf,cf->nzyxc", back, kernel, precision=lax.Precision.HIGHEST)
    filter_grad = jnp.stack(weight_taps).reshape(filters.shape)
    return out_total.astype(jnp.bfloat16), grad_total.astype(jnp.bfloat16), filter_grad
```

```python
import functools

import jax
import jax.numpy as jnp
from jax import lax
from jax.experimental import pallas as pl
from jax.experimental.pallas import tpu as pltpu
from jax.sharding import PartitionSpec as P


VMEM = pl.BlockSpec(memory_space=pltpu.VMEM)
SMEM = pl.BlockSpec(memory_space=pltpu.SMEM)
XH, ZC, YC, XL, CO = range(5)


def chan_perm(flip, step):
    return [(h * 4 + z, (h ^ flip) * 4 + (z + step) % 4) for h in range(2) for z in range(4)]


def filt_perm(step, flip, swap):
    return [
        ((y * 2 + x) * 2 + c, (((y + step) % 4) * 2 + (x ^ flip)) * 2 + (c ^ swap))
        for y in range(4)
        for x in range(2)
        for c in range(2)
    ]


def along_chan(value, flip, step):
    return lax.ppermute(value, "chan", chan_perm(flip, step))


def along_filt(value, step, flip, swap):
    return lax.ppermute(value, "filt", filt_perm(step, flip, swap))


def call(kernel, name, out_shape, in_specs, args, mib, flops=0, nbytes=1 << 20, **kw):
    return pl.pallas_call(
        kernel,
        out_shape=out_shape,
        in_specs=in_specs,
        compiler_params=pltpu.CompilerParams(vmem_limit_bytes=mib << 20),
        cost_estimate=pl.CostEstimate(flops=flops, bytes_accessed=nbytes, transcendentals=0),
        name=name,
        **kw,
    )(*args)


def rolled(rows, step):
    wide = rows.astype(jnp.float32)
    return pltpu.roll(wide, step % 16, rows.ndim - 2).astype(jnp.bfloat16)


def spread(ref, z, y, rows):
    ref[1, z, y] = rows
    ref[0, z, y] = rolled(rows, 1)
    ref[2, z, y] = rolled(rows, -1)


def close_borders(ref):
    for s in range(3):
        ref[s, :, 0] = ref[s, :, 16]
        ref[s, :, 17] = ref[s, :, 1]
    for s in range(3):
        ref[s, 0] = ref[s, 16]
        ref[s, 17] = ref[s, 1]


def build_grads(at, *refs):
    own, other, out = refs[0:4], refs[4:8], refs[8]
    for k in range(4):
        zc = (at[ZC] + 4 - k) & 3

        def plane(i, _, k=k, zc=zc):
            a, zi = i // 2, lax.rem(i, 2)
            z = (at[XH] ^ a) * 8 + zc * 2 + zi + 1
            for y in range(16):
                rows = jnp.concatenate([own[k][a, zi, y], other[k][a, zi, y]], axis=-1)
                spread(out, z, y + 1, rows)
            return 0

        lax.fori_loop(0, 4, plane, 0)
    close_borders(out)


def build_inputs(at, *refs):
    own, other, out = refs[0:4], refs[4:8], refs[8]
    for k in range(4):
        yc = (at[YC] + 4 - k) & 3
        for b in range(2):
            for part, src in enumerate((own[k], other[k])):
                y = yc * 4 + (at[XL] ^ b) * 2 + (at[CO] ^ part) + 1

                def plane(i, _, b=b, src=src, y=y):
                    a, kk = i // 4, lax.rem(i, 4)
                    for zi in range(2):
                        z = (at[XH] ^ a) * 8 + ((at[ZC] + 4 - kk) & 3) * 2 + zi + 1
                        spread(out, z, y, src[b, i, zi])
                    return 0

                lax.fori_loop(0, 8, plane, 0)
    close_borders(out)


def conv_out(step, at, x_ref, w0_ref, w1_ref, o_ref):
    zc = (at[ZC] + step) & 3
    acc = jnp.zeros((512, 256), jnp.float32)
    for tap in range(27):
        dz, dy, dx = tap // 9, (tap // 3) % 3, tap % 3
        rows = []
        for a in range(2):
            z = (at[XH] ^ a) * 8 + zc * 2 + dz
            for zi in range(2):
                rows += [x_ref[dx, z + zi, at[CO] + dy + 2 * j] for j in range(8)]
        w = jnp.concatenate([w0_ref[tap], w1_ref[tap]], axis=1)
        acc = acc + jnp.dot(jnp.concatenate(rows, 0), w, preferred_element_type=jnp.float32)
    o_ref[...] = acc.reshape(2, 2, 8, 16, 256)


def conv_grad(step, at, c_ref, w0_ref, w1_ref, o_ref):
    yc = (at[YC] + step) & 3
    acc = jnp.zeros((512, 256), jnp.float32)
    for tap in range(27):
        dz, dy, dx = tap // 9, (tap // 3) % 3, tap % 3
        rows = []
        for b in range(2):
            y = yc * 4 + (at[XL] ^ b) * 2 + at[CO] + 2 - dy
            rows.append(c_ref[2 - dx, 2 - dz : 18 - dz, y].reshape(256, 256))
        w = jnp.concatenate([w0_ref[tap], w1_ref[tap]], axis=1)
        acc = acc + lax.dot_general(
            jnp.concatenate(rows, 0),
            w,
            (((1,), (1,)), ((), ())),
            preferred_element_type=jnp.float32,
        )
    o_ref[...] = acc.reshape(2, 16, 16, 256)


def filter_kernel(at, x_ref, s0, s1, s2, s3, o_ref, ct_ref):
    @pl.when(pl.program_id(0) == 0)
    def _():
        for k, src in enumerate((s0, s1, s2, s3)):
            for a in range(2):
                for zi in range(2):
                    z = (at[XH] ^ a) * 8 + ((at[ZC] + 4 - k) & 3) * 2 + zi
                    block = src[a, zi].reshape(256, 128).astype(jnp.float32)
                    where = pl.multiple_of(z * 256, 256)
                    ct_ref[:, pl.ds(where, 256)] = block.T.astype(jnp.bfloat16)

    dz, dy = pl.program_id(0) // 3, lax.rem(pl.program_id(0), 3)
    for dx in range(3):
        r = x_ref[dx, pl.ds(dz, 16), pl.ds(dy, 16)].reshape(4096, 256)
        o_ref[dx] = jnp.dot(ct_ref[...], r, preferred_element_type=jnp.float32).T


def on_device(inputs, filters, cotangent):
    ch, fi = lax.axis_index("chan"), lax.axis_index("filt")
    xh, zc = ch // 4, ch % 4
    yc, xl, co = fi // 4, (fi // 2) % 2, fi % 2
    at = jnp.stack([xh, zc, yc, xl, co]).astype(jnp.int32)

    mine = cotangent[0]
    pair = jnp.stack([mine, along_chan(mine, 1, 0)])
    cots = [pair] + [along_chan(pair, 0, k) for k in (1, 2, 3)]
    w0 = filters.reshape(27, 256, 128)
    w1 = along_filt(w0, 0, 0, 1)
    cots_other = [along_filt(v, 0, 0, 1) for v in cots]

    flat = inputs.reshape(2, 16, 2048)
    rows = []
    for r in range(8):
        a, k = r // 4, r % 4
        to = (xh ^ a) * 4 + (zc + k) % 4
        block = lax.dynamic_slice(flat, (0, 0, to * 256), (2, 16, 256))
        rows.append(along_chan(block, a, k) if r else block)
    rows = jnp.stack(rows)
    pair_in = jnp.stack([rows, along_filt(rows, 0, 1, 0)])
    ins = [pair_in] + [along_filt(pair_in, k, 0, 0) for k in (1, 2, 3)]
    ins_other = [along_filt(v, 0, 0, 1) for v in ins]

    volume = jax.ShapeDtypeStruct((3, 18, 18, 16, 256), jnp.bfloat16)
    flops = 2 * 512 * 6912 * 256
    c3 = call(build_grads, "build_grads", volume, [SMEM] + [VMEM] * 8, [at, *cots, *cots_other], 16)
    grads = {}
    for k in (2, 1, 3, 0):
        grads[k] = call(
            functools.partial(conv_grad, k),
            f"conv_grad{k}",
            jax.ShapeDtypeStruct((2, 16, 16, 256), jnp.float32),
            [SMEM] + [VMEM] * 3,
            [at, c3, w0, w1],
            24,
            flops,
        )
    total = grads[0]
    for k in (2, 1, 3):
        total = total + along_filt(grads[k], k, 0, 0)
    input_grad = total[0] + along_filt(total[1], 0, 1, 0)
    input_grad = input_grad.astype(jnp.bfloat16).reshape(1, 16, 1, 16, 256)

    x3 = call(build_inputs, "build_inputs", volume, [SMEM] + [VMEM] * 8, [at, *ins, *ins_other], 16)
    parts = {}
    for k in (2, 1, 3, 0):
        parts[k] = call(
            functools.partial(conv_out, k),
            f"conv_out{k}",
            jax.ShapeDtypeStruct((2, 2, 8, 16, 256), jnp.float32),
            [SMEM] + [VMEM] * 3,
            [at, x3, w0, w1],
            24,
            flops,
        )
    total = parts[0]
    for k in (2, 1, 3):
        total = total + along_chan(parts[k], 0, k)
    done = (total[0] + along_chan(total[1], 1, 0)).astype(jnp.bfloat16)
    here, there = done[..., :128], along_filt(done[..., 128:], 0, 0, 1)
    even = jnp.where(co == 0, here, there)
    odd = jnp.where(co == 0, there, here)
    outputs = jnp.stack([even, odd], axis=2).reshape(1, 2, 16, 16, 128)

    filter_grad = call(
        filter_kernel,
        "filter_grad",
        jax.ShapeDtypeStruct((27, 256, 128), jnp.float32),
        [SMEM] + [VMEM] * 5,
        [at, x3, *cots],
        24,
        2 * 4096 * 27 * 256 * 128,
        grid=(9,),
        out_specs=pl.BlockSpec((3, 256, 128), lambda i: (i, 0, 0)),
        scratch_shapes=[pltpu.VMEM((128, 4096), jnp.bfloat16)],
    ).reshape(3, 3, 3, 256, 128)
    return (outputs, input_grad, filter_grad)


def solution(mesh):
    placed = (
        P(None, "chan", "filt", None, None),
        P(None, None, None, "chan", "filt"),
        P(None, "chan", None, None, "filt"),
    )
    return jax.shard_map(
        on_device,
        mesh=mesh,
        in_specs=placed,
        out_specs=(
            P(None, "chan", None, None, "filt"),
            P(None, None, "filt", None, "chan"),
            P(None, None, None, "chan", "filt"),
        ),
        check_vma=False,
    )
```

```python
import functools

import jax
import jax.numpy as jnp
from jax import lax
from jax.experimental import pallas as pl
from jax.experimental.pallas import tpu as pltpu
from jax.sharding import PartitionSpec as P


VMEM = pl.BlockSpec(memory_space=pltpu.VMEM)
SMEM = pl.BlockSpec(memory_space=pltpu.SMEM)
XH, ZC, YC, XL, CO = range(5)


def chan_perm(flip, step):
    return [(h * 4 + z, (h ^ flip) * 4 + (z + step) % 4) for h in range(2) for z in range(4)]


def filt_perm(step, flip, swap):
    return [
        ((y * 2 + x) * 2 + c, (((y + step) % 4) * 2 + (x ^ flip)) * 2 + (c ^ swap))
        for y in range(4)
        for x in range(2)
        for c in range(2)
    ]


def along_chan(value, flip, step):
    return lax.ppermute(value, "chan", chan_perm(flip, step))


def along_filt(value, step, flip, swap):
    return lax.ppermute(value, "filt", filt_perm(step, flip, swap))


def across(value, flip, swap):
    pairs = [(d, (d ^ (64 * flip)) ^ swap) for d in range(128)]
    return lax.ppermute(value, ("chan", "filt"), pairs)


def call(kernel, out_shape, in_specs, args, mib, flops=0, nbytes=1 << 20, **kw):
    return pl.pallas_call(
        kernel,
        out_shape=out_shape,
        in_specs=in_specs,
        compiler_params=pltpu.CompilerParams(vmem_limit_bytes=mib << 20),
        cost_estimate=pl.CostEstimate(flops=flops, bytes_accessed=nbytes, transcendentals=0),
        **kw,
    )(*args)


def rolled(rows, step):
    wide = rows.astype(jnp.float32)
    return pltpu.roll(wide, step % 16, rows.ndim - 2).astype(jnp.bfloat16)


def spread(ref, z, y, rows):
    ref[1, z, y] = rows
    ref[0, z, y] = rolled(rows, 1)
    ref[2, z, y] = rolled(rows, -1)


def close_borders(ref):
    for s in range(3):
        ref[s, :, 0] = ref[s, :, 16]
        ref[s, :, 17] = ref[s, :, 1]
    for s in range(3):
        ref[s, 0] = ref[s, 16]
        ref[s, 17] = ref[s, 1]


def build_grads(at, *refs):
    own, other, out = refs[0:4], refs[4:8], refs[8]
    for k in range(4):
        zc = (at[ZC] + 4 - k) & 3

        def plane(i, _, k=k, zc=zc):
            a, zi = i // 2, lax.rem(i, 2)
            z = (at[XH] ^ a) * 8 + zc * 2 + zi + 1
            for y in range(16):
                rows = jnp.concatenate([own[k][a, zi, y], other[k][a, zi, y]], axis=-1)
                spread(out, z, y + 1, rows)
            return 0

        lax.fori_loop(0, 4, plane, 0)
    close_borders(out)


def build_inputs(at, *refs):
    own, other, out = refs[0:4], refs[4:8], refs[8]
    for k in range(4):
        yc = (at[YC] + 4 - k) & 3
        for b in range(2):
            for part, src in enumerate((own[k], other[k])):
                y = yc * 4 + (at[XL] ^ b) * 2 + (at[CO] ^ part) + 1

                def plane(i, _, b=b, src=src, y=y):
                    a, kk = lax.rem(i, 2), i // 2
                    for zi in range(2):
                        z = (at[XH] ^ a) * 8 + ((at[ZC] + 4 - kk) & 3) * 2 + zi + 1
                        spread(out, z, y, src[b, kk, a, zi])
                    return 0

                lax.fori_loop(0, 8, plane, 0)
    close_borders(out)


def conv_out(step, at, x_ref, w0_ref, w1_ref, o_ref):
    zc = (at[ZC] + step) & 3
    acc = jnp.zeros((512, 256), jnp.float32)
    for tap in range(27):
        dz, dy, dx = tap // 9, (tap // 3) % 3, tap % 3
        rows = []
        for a in range(2):
            z = (at[XH] ^ a) * 8 + zc * 2 + dz
            for zi in range(2):
                rows += [x_ref[dx, z + zi, at[CO] + dy + 2 * j] for j in range(8)]
        w = jnp.concatenate([w0_ref[tap], w1_ref[tap]], axis=1)
        acc = acc + jnp.dot(jnp.concatenate(rows, 0), w, preferred_element_type=jnp.float32)
    o_ref[...] = acc.reshape(2, 2, 8, 16, 256)


def conv_grad(step, at, c_ref, w0_ref, w1_ref, o_ref):
    yc = (at[YC] + step) & 3
    acc = jnp.zeros((512, 256), jnp.float32)
    for tap in range(27):
        dz, dy, dx = tap // 9, (tap // 3) % 3, tap % 3
        rows = []
        for b in range(2):
            y = yc * 4 + (at[XL] ^ b) * 2 + at[CO] + 2 - dy
            rows.append(c_ref[2 - dx, 2 - dz : 18 - dz, y].reshape(256, 256))
        w = jnp.concatenate([w0_ref[tap], w1_ref[tap]], axis=1)
        acc = acc + lax.dot_general(
            jnp.concatenate(rows, 0),
            w,
            (((1,), (1,)), ((), ())),
            preferred_element_type=jnp.float32,
        )
    o_ref[...] = acc.reshape(2, 16, 16, 256)


def turn(at, s0, s1, s2, s3, ct_ref):
    for k, src in enumerate((s0, s1, s2, s3)):
        for a in range(2):
            for zi in range(2):
                z = (at[XH] ^ a) * 8 + ((at[ZC] + 4 - k) & 3) * 2 + zi
                block = src[a, zi].reshape(256, 128).astype(jnp.float32).T.astype(jnp.bfloat16)
                for dz in range(3):
                    where = pl.multiple_of(((z + dz + 15) & 15) * 256, 256)
                    ct_ref[dz * 128 : dz * 128 + 128, pl.ds(where, 256)] = block


def filter_kernel(dy, x_ref, ct_ref, *refs):
    o_ref = refs[-1]
    dx = pl.program_id(0)
    r = x_ref[dx, 1:17, dy : dy + 16].reshape(4096, 256)
    acc = jnp.dot(ct_ref[...], r, preferred_element_type=jnp.float32)
    for dz in range(3):
        o_ref[dz, 0] = acc[dz * 128 : dz * 128 + 128].T


def section(inputs, filters, cotangent):
    ch, fi = lax.axis_index("chan"), lax.axis_index("filt")
    xh, zc = ch // 4, ch % 4
    yc, xl, co = fi // 4, (fi // 2) % 2, fi % 2
    at = jnp.stack([xh, zc, yc, xl, co]).astype(jnp.int32)
    at, first = lax.optimization_barrier((at, co == 0))

    flat = inputs.reshape(2, 16, 2048)
    keep = lax.dynamic_slice(flat, (0, 0, xh * 1024), (2, 16, 1024))
    send = lax.dynamic_slice(flat, (0, 0, (1 - xh) * 1024), (2, 16, 1024))
    both = jnp.stack([keep, along_chan(send, 1, 0)])
    mine = cotangent[0]
    pair = jnp.stack([mine, along_chan(mine, 1, 0)])
    w0 = filters.reshape(27, 256, 128)
    w1 = along_filt(w0, 0, 0, 1)

    cots = [pair] + [along_chan(pair, 0, k) for k in (1, 2, 3)]
    cots_other = [along_filt(v, 0, 0, 1) for v in cots]

    rows = []
    for k in range(4):
        block = lax.dynamic_slice(both, (0, 0, 0, ((zc + k) % 4) * 256), (2, 2, 16, 256))
        rows.append(along_chan(block, 0, k) if k else block)
    rows = jnp.stack(rows)
    pair_in = jnp.stack([rows, along_filt(rows, 0, 1, 0)])
    ins = [pair_in] + [along_filt(pair_in, k, 0, 0) for k in (1, 2, 3)]
    ins_other = [along_filt(v, 0, 0, 1) for v in ins]

    ct = call(
        turn, jax.ShapeDtypeStruct((384, 4096), jnp.bfloat16), [SMEM] + [VMEM] * 4, [at, *cots], 4
    )
    volume = jax.ShapeDtypeStruct((3, 18, 18, 16, 256), jnp.bfloat16)
    flops = 2 * 512 * 6912 * 256
    c3 = call(build_grads, volume, [SMEM] + [VMEM] * 8, [at, *cots, *cots_other], 6)
    grads = {}
    for k in (2, 1, 3, 0):
        grads[k] = call(
            functools.partial(conv_grad, k),
            jax.ShapeDtypeStruct((2, 16, 16, 256), jnp.float32),
            [SMEM] + [VMEM] * 3,
            [at, c3, w0, w1],
            6,
            flops,
        )
    x3 = call(build_inputs, volume, [SMEM] + [VMEM] * 8, [at, *ins, *ins_other], 6)
    parts = {}
    for k in (2, 1, 3, 0):
        parts[k] = call(
            functools.partial(conv_out, k),
            jax.ShapeDtypeStruct((2, 2, 8, 16, 256), jnp.float32),
            [SMEM] + [VMEM] * 3,
            [at, x3, w0, w1],
            6,
            flops,
        )

    total = grads[0]
    for k in (2, 1, 3):
        came = along_filt(grads[k], k, 0, 0)
        total = total + came
    input_grad = total[0] + along_filt(total[1], 0, 1, 0)
    input_grad = input_grad.astype(jnp.bfloat16).reshape(1, 16, 1, 16, 256)

    total = parts[0]
    for k in (2, 1, 3):
        came = along_chan(parts[k], 0, k)
        total = total + came
    mine, rest = total[..., :128], total[..., 128:]
    here = mine[0] + across(mine[1], 1, 0)
    there = across(rest[0], 0, 1) + across(rest[1], 1, 1)
    even = jnp.where(first, here, there)
    odd = jnp.where(first, there, here)
    outputs = jnp.stack([even, odd], axis=2).astype(jnp.bfloat16).reshape(1, 2, 16, 16, 128)

    filter_grad = None
    for dy in range(3):
        kept = () if dy == 0 else (filter_grad,)
        filter_grad = call(
            functools.partial(filter_kernel, dy),
            jax.ShapeDtypeStruct((3, 9, 256, 128), jnp.float32),
            [VMEM] * 2 + [pl.BlockSpec(memory_space=pl.ANY)] * len(kept),
            [x3, ct, *kept],
            6,
            2 * 4096 * 9 * 256 * 128,
            grid=(3,),
            out_specs=pl.BlockSpec((3, 1, 256, 128), lambda i, dy=dy: (0, dy * 3 + i, 0, 0)),
            input_output_aliases={2: 0} if kept else {},
        )
    filter_grad = filter_grad.reshape(3, 3, 3, 256, 128)
    return (outputs, input_grad, filter_grad)


def solution(mesh):
    placed = (
        P(None, "chan", "filt", None, None),
        P(None, None, None, "chan", "filt"),
        P(None, "chan", None, None, "filt"),
    )
    return jax.shard_map(
        section,
        mesh=mesh,
        in_specs=placed,
        out_specs=(
            P(None, "chan", None, None, "filt"),
            P(None, None, "filt", None, "chan"),
            P(None, None, None, "chan", "filt"),
        ),
        check_vma=False,
    )
```

```python
import functools

import jax
import jax.numpy as jnp
from jax import lax
from jax.experimental import pallas as pl
from jax.experimental.pallas import tpu as pltpu
from jax.sharding import PartitionSpec as P


VMEM = pl.BlockSpec(memory_space=pltpu.VMEM)
SMEM = pl.BlockSpec(memory_space=pltpu.SMEM)
XH, ZC, YC, XL, CO = range(5)


def chan_perm(flip, step):
    return [(h * 4 + z, (h ^ flip) * 4 + (z + step) % 4) for h in range(2) for z in range(4)]


def filt_perm(step, flip, swap):
    return [
        ((y * 2 + x) * 2 + c, (((y + step) % 4) * 2 + (x ^ flip)) * 2 + (c ^ swap))
        for y in range(4)
        for x in range(2)
        for c in range(2)
    ]


def along_chan(value, flip, step):
    return lax.ppermute(value, "chan", chan_perm(flip, step))


def along_filt(value, step, flip, swap):
    return lax.ppermute(value, "filt", filt_perm(step, flip, swap))


def across(value, flip, swap):
    pairs = [(d, (d ^ (64 * flip)) ^ swap) for d in range(128)]
    return lax.ppermute(value, ("chan", "filt"), pairs)


def call(kernel, out_shape, in_specs, args, mib, flops=0, nbytes=1 << 20, **kw):
    return pl.pallas_call(
        kernel,
        out_shape=out_shape,
        in_specs=in_specs,
        compiler_params=pltpu.CompilerParams(vmem_limit_bytes=mib << 20),
        cost_estimate=pl.CostEstimate(flops=flops, bytes_accessed=nbytes, transcendentals=0),
        **kw,
    )(*args)


def rolled(rows, step):
    wide = rows.astype(jnp.float32)
    return pltpu.roll(wide, step % 16, rows.ndim - 2).astype(jnp.bfloat16)


def spread(ref, z, y, rows):
    ref[1, z, y] = rows
    ref[0, z, y] = rolled(rows, 1)
    ref[2, z, y] = rolled(rows, -1)


def close_borders(ref):
    for s in range(3):
        ref[s, :, 0] = ref[s, :, 16]
        ref[s, :, 17] = ref[s, :, 1]
    for s in range(3):
        ref[s, 0] = ref[s, 16]
        ref[s, 17] = ref[s, 1]


def build_grads(at, *refs):
    own, other, out = refs[0:4], refs[4:8], refs[8]
    for k in range(4):
        zc = (at[ZC] + 4 - k) & 3

        def plane(i, _, k=k, zc=zc):
            a, zi = i // 2, lax.rem(i, 2)
            z = (at[XH] ^ a) * 8 + zc * 2 + zi + 1
            for y in range(16):
                rows = jnp.concatenate([own[k][a, zi, y], other[k][a, zi, y]], axis=-1)
                spread(out, z, y + 1, rows)
            return 0

        lax.fori_loop(0, 4, plane, 0)
    close_borders(out)


def build_inputs(at, *refs):
    own, other, out = refs[0:4], refs[4:8], refs[8]
    for k in range(4):
        yc = (at[YC] + 4 - k) & 3
        for b in range(2):
            for part, src in enumerate((own[k], other[k])):
                y = yc * 4 + (at[XL] ^ b) * 2 + (at[CO] ^ part) + 1

                def plane(i, _, b=b, src=src, y=y):
                    a, kk = lax.rem(i, 2), i // 2
                    for zi in range(2):
                        z = (at[XH] ^ a) * 8 + ((at[ZC] + 4 - kk) & 3) * 2 + zi + 1
                        spread(out, z, y, src[b, kk, a, zi])
                    return 0

                lax.fori_loop(0, 8, plane, 0)
    close_borders(out)


def conv_out(steps, at, x_ref, w0_ref, w1_ref, *o_refs):
    acc = jnp.zeros((512 * len(steps), 256), jnp.float32)
    for tap in range(27):
        dz, dy, dx = tap // 9, (tap // 3) % 3, tap % 3
        rows = []
        for step in steps:
            for a in range(2):
                z = (at[XH] ^ a) * 8 + ((at[ZC] + step) & 3) * 2 + dz
                for zi in range(2):
                    rows += [x_ref[dx, z + zi, at[CO] + dy + 2 * j] for j in range(8)]
        w = jnp.concatenate([w0_ref[tap], w1_ref[tap]], axis=1)
        acc = acc + jnp.dot(jnp.concatenate(rows, 0), w, preferred_element_type=jnp.float32)
    for n, o_ref in enumerate(o_refs):
        o_ref[...] = acc[512 * n : 512 * n + 512].reshape(2, 2, 8, 16, 256)


def conv_grad(steps, at, c_ref, w0_ref, w1_ref, *o_refs):
    acc = jnp.zeros((512 * len(steps), 256), jnp.float32)
    for tap in range(27):
        dz, dy, dx = tap // 9, (tap // 3) % 3, tap % 3
        rows = []
        for step in steps:
            for b in range(2):
                y = ((at[YC] + step) & 3) * 4 + (at[XL] ^ b) * 2 + at[CO] + 2 - dy
                rows.append(c_ref[2 - dx, 2 - dz : 18 - dz, y].reshape(256, 256))
        w = jnp.concatenate([w0_ref[tap], w1_ref[tap]], axis=1)
        acc = acc + lax.dot_general(
            jnp.concatenate(rows, 0),
            w,
            (((1,), (1,)), ((), ())),
            preferred_element_type=jnp.float32,
        )
    for n, o_ref in enumerate(o_refs):
        o_ref[...] = acc[512 * n : 512 * n + 512].reshape(2, 16, 16, 256)


def turn(at, s0, s1, s2, s3, ct_ref):
    for k, src in enumerate((s0, s1, s2, s3)):
        for a in range(2):
            for zi in range(2):
                z = (at[XH] ^ a) * 8 + ((at[ZC] + 4 - k) & 3) * 2 + zi
                block = src[a, zi].reshape(256, 128).astype(jnp.float32).T.astype(jnp.bfloat16)
                for dz in range(3):
                    where = pl.multiple_of(((z + dz + 15) & 15) * 256, 256)
                    ct_ref[dz * 128 : dz * 128 + 128, pl.ds(where, 256)] = block


def filter_kernel(dy, x_ref, ct_ref, *refs):
    o_ref = refs[-1]
    for dx in range(3):
        r = x_ref[dx, 1:17, dy : dy + 16].reshape(4096, 256)
        acc = jnp.dot(ct_ref[...], r, preferred_element_type=jnp.float32)
        for dz in range(3):
            o_ref[dz, dx] = acc[dz * 128 : dz * 128 + 128].T


def finish(kept, came, o_ref):
    o_ref[...] = (kept[0] + came[...]).astype(jnp.bfloat16)


def convolve(kernel, shape, args):
    chunks = {}
    for steps in ((1, 3), (2,), (0,)):
        made = call(
            functools.partial(kernel, steps),
            [jax.ShapeDtypeStruct(shape, jnp.float32)] * len(steps),
            [SMEM] + [VMEM] * 3,
            args,
            8,
            2 * 512 * len(steps) * 6912 * 256,
        )
        chunks.update(zip(steps, made))
    return chunks


def section(inputs, filters, cotangent):
    ch, fi = lax.axis_index("chan"), lax.axis_index("filt")
    xh, zc = ch // 4, ch % 4
    yc, xl, co = fi // 4, (fi // 2) % 2, fi % 2
    at = jnp.stack([xh, zc, yc, xl, co]).astype(jnp.int32)
    at, first = lax.optimization_barrier((at, co == 0))

    flat = inputs.reshape(2, 16, 2048)
    keep = lax.dynamic_slice(flat, (0, 0, xh * 1024), (2, 16, 1024))
    send = lax.dynamic_slice(flat, (0, 0, (1 - xh) * 1024), (2, 16, 1024))
    both = jnp.stack([keep, along_chan(send, 1, 0)])
    mine = cotangent[0]
    pair = jnp.stack([mine, along_chan(mine, 1, 0)])
    w0 = filters.reshape(27, 256, 128)
    w1 = along_filt(w0, 0, 0, 1)

    cots = [pair] + [along_chan(pair, 0, k) for k in (1, 2, 3)]
    cots_other = [along_filt(v, 0, 0, 1) for v in cots]

    rows = []
    for k in range(4):
        block = lax.dynamic_slice(both, (0, 0, 0, ((zc + k) % 4) * 256), (2, 2, 16, 256))
        rows.append(along_chan(block, 0, k) if k else block)
    rows = jnp.stack(rows)
    pair_in = jnp.stack([rows, along_filt(rows, 0, 1, 0)])
    ins = [pair_in] + [along_filt(pair_in, k, 0, 0) for k in (1, 2, 3)]
    ins_other = [along_filt(v, 0, 0, 1) for v in ins]

    ct = call(
        turn, jax.ShapeDtypeStruct((384, 4096), jnp.bfloat16), [SMEM] + [VMEM] * 4, [at, *cots], 4
    )
    volume = jax.ShapeDtypeStruct((3, 18, 18, 16, 256), jnp.bfloat16)
    c3 = call(build_grads, volume, [SMEM] + [VMEM] * 8, [at, *cots, *cots_other], 6)
    grads = convolve(conv_grad, (2, 16, 16, 256), [at, c3, w0, w1])
    x3 = call(build_inputs, volume, [SMEM] + [VMEM] * 8, [at, *ins, *ins_other], 6)
    parts = convolve(conv_out, (2, 2, 8, 16, 256), [at, x3, w0, w1])

    total = grads[0]
    for k in (2, 1, 3):
        came = along_filt(grads[k], k, 0, 0)
        total = total + came
    came = along_filt(total[1], 0, 1, 0)
    narrow = jax.ShapeDtypeStruct((16, 16, 256), jnp.bfloat16)
    input_grad = call(finish, narrow, [VMEM] * 2, [total, came], 4)
    input_grad = input_grad.reshape(1, 16, 1, 16, 256)

    total = parts[0]
    for k in (2, 1, 3):
        came = along_chan(parts[k], 0, k)
        total = total + came
    mine, rest = total[..., :128], total[..., 128:]
    here = mine[0] + across(mine[1], 1, 0)
    there = across(rest[0], 0, 1) + across(rest[1], 1, 1)
    even = jnp.where(first, here, there)
    odd = jnp.where(first, there, here)
    outputs = jnp.stack([even, odd], axis=2).astype(jnp.bfloat16).reshape(1, 2, 16, 16, 128)

    filter_grad = None
    for dy in range(3):
        kept = () if dy == 0 else (filter_grad,)
        filter_grad = call(
            functools.partial(filter_kernel, dy),
            jax.ShapeDtypeStruct((3, 9, 256, 128), jnp.float32),
            [VMEM] * 2 + [pl.BlockSpec(memory_space=pl.ANY)] * len(kept),
            [x3, ct, *kept],
            6,
            2 * 4096 * 9 * 256 * 128,
            grid=(1,),
            out_specs=pl.BlockSpec((3, 3, 256, 128), lambda i, dy=dy: (0, dy, 0, 0)),
            input_output_aliases={2: 0} if kept else {},
        )
    filter_grad = filter_grad.reshape(3, 3, 3, 256, 128)
    return (outputs, input_grad, filter_grad)


def solution(mesh):
    placed = (
        P(None, "chan", "filt", None, None),
        P(None, None, None, "chan", "filt"),
        P(None, "chan", None, None, "filt"),
    )
    return jax.shard_map(
        section,
        mesh=mesh,
        in_specs=placed,
        out_specs=(
            P(None, "chan", None, None, "filt"),
            P(None, None, "filt", None, "chan"),
            P(None, None, None, "chan", "filt"),
        ),
        check_vma=False,
    )
```

```python
import functools

import jax
import jax.numpy as jnp
from jax import lax
from jax.experimental import pallas as pl
from jax.experimental.pallas import tpu as pltpu
from jax.sharding import PartitionSpec as P


VMEM = pl.BlockSpec(memory_space=pltpu.VMEM)
SMEM = pl.BlockSpec(memory_space=pltpu.SMEM)
XH, ZC, YC, XL, CO = range(5)


def chan_perm(flip, step):
    return [(h * 4 + z, (h ^ flip) * 4 + (z + step) % 4) for h in range(2) for z in range(4)]


def filt_perm(step, flip, swap):
    return [
        ((y * 2 + x) * 2 + c, (((y + step) % 4) * 2 + (x ^ flip)) * 2 + (c ^ swap))
        for y in range(4)
        for x in range(2)
        for c in range(2)
    ]


def along_chan(value, flip, step):
    return lax.ppermute(value, "chan", chan_perm(flip, step))


def along_filt(value, step, flip, swap):
    return lax.ppermute(value, "filt", filt_perm(step, flip, swap))


def across(value, flip, swap):
    pairs = [(d, (d ^ (64 * flip)) ^ swap) for d in range(128)]
    return lax.ppermute(value, ("chan", "filt"), pairs)


def call(kernel, out_shape, in_specs, args, mib, flops=0, nbytes=1 << 20, **kw):
    return pl.pallas_call(
        kernel,
        out_shape=out_shape,
        in_specs=in_specs,
        compiler_params=pltpu.CompilerParams(vmem_limit_bytes=mib << 20),
        cost_estimate=pl.CostEstimate(flops=flops, bytes_accessed=nbytes, transcendentals=0),
        **kw,
    )(*args)


def rolled(rows, step):
    wide = rows.astype(jnp.float32)
    return pltpu.roll(wide, step % 16, rows.ndim - 2).astype(jnp.bfloat16)


def spread(ref, z, y, rows):
    ref[1, z, y] = rows
    ref[0, z, y] = rolled(rows, 1)
    ref[2, z, y] = rolled(rows, -1)


def close_borders(ref):
    for s in range(3):
        ref[s, :, 0] = ref[s, :, 16]
        ref[s, :, 17] = ref[s, :, 1]
    for s in range(3):
        ref[s, 0] = ref[s, 16]
        ref[s, 17] = ref[s, 1]


def build_grads(at, *refs):
    own, other, out = refs[0:4], refs[4:8], refs[8]
    for k in range(4):
        zc = (at[ZC] + 4 - k) & 3

        def plane(i, _, k=k, zc=zc):
            a, zi = i // 2, lax.rem(i, 2)
            z = (at[XH] ^ a) * 8 + zc * 2 + zi + 1
            for y in range(16):
                rows = jnp.concatenate([own[k][a, zi, y], other[k][a, zi, y]], axis=-1)
                spread(out, z, y + 1, rows)
            return 0

        lax.fori_loop(0, 4, plane, 0)
    close_borders(out)


def build_inputs(at, *refs):
    own, other, out = refs[0:4], refs[4:8], refs[8]
    for k in range(4):
        yc = (at[YC] + 4 - k) & 3
        for b in range(2):
            for part, src in enumerate((own[k], other[k])):
                y = yc * 4 + (at[XL] ^ b) * 2 + (at[CO] ^ part) + 1

                def plane(i, _, b=b, src=src, y=y):
                    a, kk = lax.rem(i, 2), i // 2
                    for zi in range(2):
                        z = (at[XH] ^ a) * 8 + ((at[ZC] + 4 - kk) & 3) * 2 + zi + 1
                        spread(out, z, y, src[b, kk, a, zi])
                    return 0

                lax.fori_loop(0, 8, plane, 0)
    close_borders(out)


def conv_out(steps, at, x_ref, w0_ref, w1_ref, *o_refs):
    acc = jnp.zeros((512 * len(steps), 256), jnp.float32)
    for tap in range(27):
        dz, dy, dx = tap // 9, (tap // 3) % 3, tap % 3
        rows = []
        for step in steps:
            for a in range(2):
                z = (at[XH] ^ a) * 8 + ((at[ZC] + step) & 3) * 2 + dz
                for zi in range(2):
                    rows += [x_ref[dx, z + zi, at[CO] + dy + 2 * j] for j in range(8)]
        w = jnp.concatenate([w0_ref[tap], w1_ref[tap]], axis=1)
        acc = acc + jnp.dot(jnp.concatenate(rows, 0), w, preferred_element_type=jnp.float32)
    for n, o_ref in enumerate(o_refs):
        o_ref[...] = acc[512 * n : 512 * n + 512].reshape(2, 2, 8, 16, 256)


def conv_grad(steps, at, c_ref, w0_ref, w1_ref, *o_refs):
    acc = jnp.zeros((512 * len(steps), 256), jnp.float32)
    for tap in range(27):
        dz, dy, dx = tap // 9, (tap // 3) % 3, tap % 3
        rows = []
        for step in steps:
            for b in range(2):
                y = ((at[YC] + step) & 3) * 4 + (at[XL] ^ b) * 2 + at[CO] + 2 - dy
                rows.append(c_ref[2 - dx, 2 - dz : 18 - dz, y].reshape(256, 256))
        w = jnp.concatenate([w0_ref[tap], w1_ref[tap]], axis=1)
        acc = acc + lax.dot_general(
            jnp.concatenate(rows, 0),
            w,
            (((1,), (1,)), ((), ())),
            preferred_element_type=jnp.float32,
        )
    for n, o_ref in enumerate(o_refs):
        o_ref[...] = acc[512 * n : 512 * n + 512].reshape(2, 16, 16, 256)


def turn(at, s0, s1, s2, s3, ct_ref):
    for k, src in enumerate((s0, s1, s2, s3)):
        for a in range(2):
            for zi in range(2):
                z = (at[XH] ^ a) * 8 + ((at[ZC] + 4 - k) & 3) * 2 + zi
                block = src[a, zi].reshape(256, 128).astype(jnp.float32).T.astype(jnp.bfloat16)
                for dz in range(3):
                    where = pl.multiple_of(((z + dz + 15) & 15) * 256, 256)
                    ct_ref[dz * 128 : dz * 128 + 128, pl.ds(where, 256)] = block


def filter_kernel(dy, x_ref, ct_ref, *refs):
    o_ref = refs[-1]
    for dx in range(3):
        r = x_ref[dx, 1:17, dy : dy + 16].reshape(4096, 256)
        acc = jnp.dot(ct_ref[...], r, preferred_element_type=jnp.float32)
        for dz in range(3):
            o_ref[dz, dx] = acc[dz * 128 : dz * 128 + 128].T


def finish(kept, came, o_ref):
    o_ref[...] = (kept[0] + came[...]).astype(jnp.bfloat16)


def convolve(kernel, shape, args, groups):
    chunks = {}
    for steps in groups:
        made = call(
            functools.partial(kernel, steps),
            [jax.ShapeDtypeStruct(shape, jnp.float32)] * len(steps),
            [SMEM] + [VMEM] * 3,
            args,
            8,
            2 * 512 * len(steps) * 6912 * 256,
        )
        chunks.update(zip(steps, made))
    return chunks


def section(inputs, filters, cotangent):
    ch, fi = lax.axis_index("chan"), lax.axis_index("filt")
    xh, zc = ch // 4, ch % 4
    yc, xl, co = fi // 4, (fi // 2) % 2, fi % 2
    at = jnp.stack([xh, zc, yc, xl, co]).astype(jnp.int32)
    at, first = lax.optimization_barrier((at, co == 0))

    flat = inputs.reshape(2, 16, 2048)
    keep = lax.dynamic_slice(flat, (0, 0, xh * 1024), (2, 16, 1024))
    send = lax.dynamic_slice(flat, (0, 0, (1 - xh) * 1024), (2, 16, 1024))
    both = jnp.stack([keep, along_chan(send, 1, 0)])
    mine = cotangent[0]
    pair = jnp.stack([mine, along_chan(mine, 1, 0)])
    w0 = filters.reshape(27, 256, 128)
    w1 = along_filt(w0, 0, 0, 1)

    cots = [pair] + [along_chan(pair, 0, k) for k in (1, 2, 3)]
    cots_other = [along_filt(v, 0, 0, 1) for v in cots]

    rows = []
    for k in range(4):
        block = lax.dynamic_slice(both, (0, 0, 0, ((zc + k) % 4) * 256), (2, 2, 16, 256))
        rows.append(along_chan(block, 0, k) if k else block)
    rows = jnp.stack(rows)
    pair_in = jnp.stack([rows, along_filt(rows, 0, 1, 0)])
    ins = [pair_in] + [along_filt(pair_in, k, 0, 0) for k in (1, 2, 3)]
    ins_other = [along_filt(v, 0, 0, 1) for v in ins]

    ct = call(
        turn, jax.ShapeDtypeStruct((384, 4096), jnp.bfloat16), [SMEM] + [VMEM] * 4, [at, *cots], 4
    )
    volume = jax.ShapeDtypeStruct((3, 18, 18, 16, 256), jnp.bfloat16)
    c3 = call(build_grads, volume, [SMEM] + [VMEM] * 8, [at, *cots, *cots_other], 6)
    grads = convolve(conv_grad, (2, 16, 16, 256), [at, c3, w0, w1], ((1, 3), (2,), (0,)))
    x3 = call(build_inputs, volume, [SMEM] + [VMEM] * 8, [at, *ins, *ins_other], 6)
    parts = convolve(conv_out, (2, 2, 8, 16, 256), [at, x3, w0, w1], ((1, 3), (2, 0)))

    total = grads[0]
    for k in (2, 1, 3):
        came = along_filt(grads[k], k, 0, 0)
        total = total + came
    came = along_filt(total[1], 0, 1, 0)
    narrow = jax.ShapeDtypeStruct((16, 16, 256), jnp.bfloat16)
    input_grad = call(finish, narrow, [VMEM] * 2, [total, came], 4)
    input_grad = input_grad.reshape(1, 16, 1, 16, 256)

    total = parts[0]
    for k in (2, 1, 3):
        came = along_chan(parts[k], 0, k)
        total = total + came
    mine, rest = total[..., :128], total[..., 128:]
    here = mine[0] + across(mine[1], 1, 0)
    there = across(rest[0], 0, 1) + across(rest[1], 1, 1)
    even = jnp.where(first, here, there)
    odd = jnp.where(first, there, here)
    outputs = jnp.stack([even, odd], axis=2).astype(jnp.bfloat16).reshape(1, 2, 16, 16, 128)

    filter_grad = None
    for dy in range(3):
        kept = () if dy == 0 else (filter_grad,)
        filter_grad = call(
            functools.partial(filter_kernel, dy),
            jax.ShapeDtypeStruct((3, 9, 256, 128), jnp.float32),
            [VMEM] * 2 + [pl.BlockSpec(memory_space=pl.ANY)] * len(kept),
            [x3, ct, *kept],
            6,
            2 * 4096 * 9 * 256 * 128,
            grid=(1,),
            out_specs=pl.BlockSpec((3, 3, 256, 128), lambda i, dy=dy: (0, dy, 0, 0)),
            input_output_aliases={2: 0} if kept else {},
        )
    filter_grad = filter_grad.reshape(3, 3, 3, 256, 128)
    return (outputs, input_grad, filter_grad)


def solution(mesh):
    placed = (
        P(None, "chan", "filt", None, None),
        P(None, None, None, "chan", "filt"),
        P(None, "chan", None, None, "filt"),
    )
    return jax.shard_map(
        section,
        mesh=mesh,
        in_specs=placed,
        out_specs=(
            P(None, "chan", None, None, "filt"),
            P(None, None, "filt", None, "chan"),
            P(None, None, None, "chan", "filt"),
        ),
        check_vma=False,
    )
```
